256 devices in a mesh: drive: 4 (over y), brick: 64 (over x, z, core).
Axes of the slice: x: 4, y: 4, z: 8, core: 2. Of those that a mesh axis runs over, the one named last changes fastest.
Arguments:
- cam_tiles: bfloat16 [4, 1, 256, 64, 256], P('drive', None, 'brick')
- vox_embed: bfloat16 [1536, 128, 256], P('brick'), may hold values from -6 to 6
- prev_state: bfloat16 [4, 1536, 128, 256], P('drive', 'brick'), may hold values from -6 to 6
- tile_sends: int32 [4, 1, 64, 128], P('drive', None, 'brick'), may hold values from 0 to 3, as said below
- brick_tiles: int32 [4, 1, 1536, 8], P('drive', None, 'brick'), may hold values from -1 to 127, as said below
- ego_shift: int32 [4, 1], P('drive'), may hold values from 0 to 24
- norm_gains: float32 [2, 256], replicated, may hold values from 0.1 to 1.9
- w_query: bfloat16 [256, 256], replicated, may hold values from -0.375 to 0.375
- w_keyval: bfloat16 [256, 512], replicated, may hold values from -0.375 to 0.375
- w_attn_out: bfloat16 [256, 256], replicated, may hold values from -0.375 to 0.375
- w_in: bfloat16 [256, 512], replicated, may hold values from -0.375 to 0.375
- w_out: bfloat16 [512, 256], replicated, may hold values from -0.25 to 0.25
- grad_out: bfloat16 [4, 1536, 128, 256], P('drive', 'brick'), may hold values from -0.015625 to 0.015625
Outputs:
- new_state: bfloat16 [4, 1536, 128, 256], P('drive', 'brick')
- grad_w_in: float32 [256, 512], replicated
- grad_w_out: float32 [512, 256], replicated
The draws below stay inside these ranges and needn't reach their ends.
Inputs may be any that keep to these rules, and one draw needn't show every extreme that they name: `tile_sends`: entry [drive, frame, p, d * 2 + c] is a tile of shard p, a local index, that shard p sends to shard d as its c-th slot; the 2 entries of one pair are distinct. `brick_tiles`: -1 is padding; other entries are distinct within a brick and name received slots; every brick has one or more, and in each drive and frame some brick has all 8.
All inputs are finite; a program needn't handle non-finite values.
Results may differ from the reference program's by a relative error of at most 0.0022.
The reference program's roundings to bfloat16 on the way count: a program that leaves them out, or rounds other values in their place, can miss the bound.
Values may be sent and summed in bfloat16 or wider, within the bound.
No kernel may reach another device: no remote copies, remote signals or barrier semaphores. Data moves between devices by JAX's collectives and lax.ppermute only.
A program may use at most 128 MiB of HBM per device.

```python
import jax
import jax.numpy as jnp
from jax import lax

C = 256
FF = 512
HD = 32
PIX = 64
L = 8
CAP = 2
BRICK = 128
FRAMES = 1
TILE_DEV = 4
BRICK_DEV = 24
DRIVES = 4
SHARDS = 64
SLOTS = 128
TILES = 256
BRICKS = 1536


def routing_plan(key):
    base_key = jax.random.fold_in(key, 1009)
    key_counts, key_offset, key_tiles, key_slots, key_want, key_full = jax.random.split(base_key, 6)
    leading = (DRIVES, FRAMES)
    counts = jax.random.randint(key_counts, leading + (SHARDS, SHARDS), 0, CAP + 1)
    offset = jax.random.randint(key_offset, leading + (SHARDS, 1), 0, SHARDS)
    target = jnp.arange(SHARDS)[:, None]
    sender = jnp.arange(SHARDS)[None, :]
    needed = (L + CAP - 1) // CAP
    counts = jnp.where((sender - target - offset) % SHARDS < needed, CAP, counts)
    tile_scores = jax.random.randint(key_tiles, leading + (SHARDS, SHARDS, TILE_DEV), 0, 1 << 20) * TILE_DEV + jnp.arange(TILE_DEV)
    chosen = jnp.argsort(tile_scores, axis=-1)[..., :CAP]
    sends = chosen.reshape(leading + (SHARDS, SHARDS * CAP)).astype(jnp.int32)
    used = (jnp.arange(CAP) < counts[..., None]).reshape(leading + (SHARDS, SLOTS))
    penalty = jnp.where(used, 0, (1 << 20) * SLOTS)
    slot_scores = jax.random.randint(key_slots, leading + (SHARDS, BRICK_DEV, SLOTS), 0, 1 << 20) * SLOTS + jnp.arange(SLOTS) + penalty[..., None, :]
    picked = jnp.argsort(slot_scores, axis=-1)[..., :L]
    used_count = jnp.sum(used.astype(jnp.int32), axis=-1)
    wanted = jax.random.randint(key_want, leading + (SHARDS, BRICK_DEV), 1, L + 1)
    full_brick = jax.random.randint(key_full, leading + (SHARDS, 1), 0, BRICK_DEV)
    wanted = jnp.where(jnp.arange(BRICK_DEV) == full_brick, L, wanted)
    live_count = jnp.minimum(wanted, used_count[..., None])
    lists = jnp.where(jnp.arange(L) < live_count[..., None], picked, -1)
    lists = lists.reshape(leading + (SHARDS * BRICK_DEV, L)).astype(jnp.int32)
    return (sends, lists)


def draw_tile_sends(key, part):
    return routing_plan(key)[0]


def draw_brick_tiles(key, part):
    return routing_plan(key)[1]


def draw_ego_shift(key, part):
    key_value, key_pick = jax.random.split(jax.random.fold_in(key, 23))
    total = DRIVES * FRAMES
    values = jax.random.randint(key_value, (total,), 0, BRICK_DEV + 1)
    forced = jax.random.randint(key_pick, (), 0, total)
    positions = jnp.arange(total)
    values = jnp.where(positions == forced, BRICK_DEV, values)
    return values.reshape(DRIVES, FRAMES).astype(jnp.int32)


def draw_cam_tiles(key, part):
    key_base = jax.random.fold_in(jax.random.fold_in(key, 31), 0)
    shape = (DRIVES, FRAMES, TILES, PIX, C)
    base = jax.random.normal(key_base, shape, jnp.float32)
    return base.astype(jnp.bfloat16)


def block_scale(own_key, extent, cuts, smallest, high):
    def one(axis_at, parts):
        heights = jax.random.uniform(jax.random.fold_in(jax.random.fold_in(own_key, 6), axis_at), (parts,), jnp.float32, smallest / len(cuts), high / len(cuts))
        return jnp.repeat(jnp.exp(heights), extent[axis_at] // parts).reshape((-1,) + (1,) * (len(extent) - axis_at - 1))

    factor_of = one(*cuts[0])
    for cut in cuts[1:]:
        factor_of = factor_of * one(*cut)
    return factor_of


def noise(stream_key, shape, deviation, most, shards=(), kind=jnp.bfloat16):
    values = deviation * jax.random.normal(stream_key, shape, jnp.float32)
    if shards:
        values = values * block_scale(stream_key, shape, shards, -0.22, 0.18)
    return jnp.clip(values, -most, most).astype(kind)


def setup_inputs(seed: int = 0) -> dict:
    seeds = jax.random.split(jax.random.key(seed), 14)
    return {
        "cam_tiles": draw_cam_tiles(jax.random.fold_in(seeds[13], 71), 0),
        "vox_embed": noise(seeds[1], (BRICKS, BRICK, C), 1.0, 6.0, ((0, 64),)),
        "prev_state": noise(seeds[2], (DRIVES, BRICKS, BRICK, C), 1.0, 6.0, ((0, 4), (1, 64))),
        "tile_sends": draw_tile_sends(jax.random.fold_in(seeds[13], 71), 0),
        "brick_tiles": draw_brick_tiles(jax.random.fold_in(seeds[13], 71), 0),
        "ego_shift": draw_ego_shift(jax.random.fold_in(seeds[13], 71), 0),
        "norm_gains": jnp.clip(1.0 + 0.18 * jax.random.normal(seeds[6], (2, C), jnp.float32), 0.1, 1.9),
        "w_query": noise(seeds[7], (C, C), C ** -0.5, 0.375),
        "w_keyval": noise(seeds[8], (C, 2 * C), C ** -0.5, 0.375),
        "w_attn_out": noise(seeds[9], (C, C), C ** -0.5, 0.375),
        "w_in": noise(seeds[10], (C, FF), C ** -0.5, 0.375),
        "w_out": noise(seeds[11], (FF, C), FF ** -0.5, 0.25),
        "grad_out": noise(seeds[12], (DRIVES, BRICKS, BRICK, C), (1.0 / (DRIVES * BRICKS * BRICK) ** 0.5), 0.015625, ((0, 4), (1, 64))),
    }


def rms_norm(values, norm_gain):
    mean_sq = lax.optimization_barrier(jnp.mean(values * values, axis=-1, keepdims=True))
    return values * lax.rsqrt(mean_sq + 1e-06) * norm_gain

def gelu_tanh(values):
    return jax.nn.gelu(values, approximate=True)

def reference(cam_tiles, vox_embed, prev_state, tile_sends, brick_tiles, ego_shift, norm_gains, w_query, w_keyval, w_attn_out, w_in, w_out, grad_out):
    head_count = C // HD
    scale = 1.0 / HD ** 0.5
    group_size = min(BRICK_DEV, max(1, 512 // BRICK))
    blocks = BRICKS // group_size
    sum_w_in = jnp.zeros((C, FF), jnp.float32)
    sum_w_out = jnp.zeros((FF, C), jnp.float32)
    states = []
    for drive_idx in range(DRIVES):
        voxel_state = prev_state[drive_idx]
        for frame_idx in range(FRAMES):
            padded = jnp.concatenate([jnp.zeros((BRICK_DEV, BRICK, C), voxel_state.dtype), voxel_state], 0)
            start = (BRICK_DEV - ego_shift[drive_idx, frame_idx]).astype(jnp.int32)
            shifted = lax.dynamic_slice_in_dim(padded, start, BRICKS, 0)
            q_in = vox_embed.astype(jnp.float32) + shifted.astype(jnp.float32)
            normed = rms_norm(q_in, norm_gains[0]).astype(jnp.bfloat16)
            queries = jnp.dot(normed.reshape(-1, C), w_query, preferred_element_type=jnp.float32).astype(jnp.bfloat16)
            keyval = jnp.dot(cam_tiles[drive_idx, frame_idx].reshape(-1, C), w_keyval, preferred_element_type=jnp.float32).astype(jnp.bfloat16).reshape(TILES, PIX, 2 * C)
            entries = brick_tiles[drive_idx, frame_idx]
            clipped = jnp.maximum(entries, 0)
            source = clipped // CAP
            column = (jnp.arange(BRICKS, dtype=jnp.int32) // BRICK_DEV)[:, None] * CAP + clipped % CAP
            local_ids = tile_sends[drive_idx, frame_idx][source, column]
            tile_ids = (source * TILE_DEV + local_ids).astype(jnp.int32)
            query_blocks = queries.reshape(blocks, group_size, BRICK, head_count, HD)

            def attend(operands):
                query_block, id_block, entry_block = operands
                gathered = keyval[id_block].reshape(group_size, L * PIX, 2, head_count, HD).astype(jnp.float32)
                keys_part = gathered[:, :, 0]
                values_part = gathered[:, :, 1]
                scores = jnp.einsum('gqhd,gkhd->ghqk', query_block.astype(jnp.float32), keys_part) * scale
                live_keys = jnp.broadcast_to((entry_block >= 0)[:, :, None], (group_size, L, PIX)).reshape(group_size, 1, 1, L * PIX)
                scores = jnp.where(live_keys, scores, -1e+30)
                row_peak = lax.optimization_barrier(jnp.max(scores, axis=-1, keepdims=True))
                raised = jnp.exp(scores - row_peak)
                weights = (raised / lax.optimization_barrier(jnp.sum(raised, axis=-1, keepdims=True))).astype(jnp.bfloat16)
                mixed = jnp.einsum('ghqk,gkhd->gqhd', weights.astype(jnp.float32), values_part)
                return mixed.astype(jnp.bfloat16)
            attended = lax.map(attend, (query_blocks, tile_ids.reshape(blocks, group_size, L), entries.reshape(blocks, group_size, L))).reshape(-1, C)
            residual_x = q_in.reshape(-1, C) + jnp.dot(attended, w_attn_out, preferred_element_type=jnp.float32)
            hidden_in = rms_norm(residual_x, norm_gains[1]).astype(jnp.bfloat16)
            pre_act = jnp.dot(hidden_in, w_in, preferred_element_type=jnp.float32)
            activated = gelu_tanh(pre_act).astype(jnp.bfloat16)
            voxel_state = (residual_x + jnp.dot(activated, w_out, preferred_element_type=jnp.float32)).astype(jnp.bfloat16).reshape(BRICKS, BRICK, C)
        states.append(voxel_state)
        cotangent = grad_out[drive_idx].reshape(-1, C)
        sum_w_out = sum_w_out + jnp.dot(activated.T, cotangent, preferred_element_type=jnp.float32)
        d_act = jnp.dot(cotangent, w_out.T, preferred_element_type=jnp.float32)
        unused_value, pullback = jax.vjp(gelu_tanh, pre_act)
        d_pre = pullback(d_act)[0].astype(jnp.bfloat16)
        sum_w_in = sum_w_in + jnp.dot(hidden_in.T, d_pre, preferred_element_type=jnp.float32)
    return (jnp.stack(states), sum_w_in, sum_w_out)
```

```python
import functools

import jax
import jax.numpy as jnp
from jax import lax
from jax.experimental import pallas as pl
from jax.experimental.pallas import tpu as pltpu
from jax.sharding import PartitionSpec as P

HD = 32
GROUP = 4
NT = (((1,), (1,)), ((), ()))
TN = (((0,), (0,)), ((), ()))


def dot(a, b, dims=(((1,), (0,)), ((), ()))):
    return lax.dot_general(a, b, dims, preferred_element_type=jnp.float32)


def rms_norm(values, norm_gain):
    mean_sq = jnp.mean(values * values, axis=-1, keepdims=True)
    return values * lax.rsqrt(mean_sq + 1e-06) * norm_gain


def step_kernel(
    sends,
    entries,
    shift,
    cams,
    behind,
    prev,
    vox,
    cot,
    gains,
    w_query,
    w_key,
    w_value_t,
    w_attn_out,
    w_in,
    w_out,
    new_state,
    grad_in,
    grad_out,
    qin_s,
    query_s,
    att_s,
    feat_s,
):
    step = pl.program_id(0)
    bricks = prev.shape[0]
    size = prev.shape[1]
    width = prev.shape[2]
    list_len = entries.shape[0] // bricks
    pixels = cams.shape[1]
    tile_dev = cams.shape[0] // (sends.shape[0] // 2)
    rows = GROUP * size
    log2_scale = 1.4426950408889634 / HD**0.5

    @pl.when(step == 0)
    def _():
        grad_in[...] = jnp.zeros_like(grad_in)
        grad_out[...] = jnp.zeros_like(grad_out)
        feat_s[...] = jnp.zeros_like(feat_s)

    start = bricks - shift[0]
    for g in range(GROUP):
        at = start + step * GROUP + g
        from_behind = behind[jnp.minimum(at, bricks - 1)].astype(jnp.float32)
        from_own = prev[jnp.maximum(at - bricks, 0)].astype(jnp.float32)
        shifted = jnp.where(at < bricks, from_behind, from_own)
        q_in = vox[g].astype(jnp.float32) + shifted
        here = pl.ds(g * size, size)
        qin_s[here, :] = q_in
        normed = rms_norm(q_in, gains[0:1, :]).astype(jnp.bfloat16)
        query_s[here, :] = dot(normed, w_query[...]).astype(jnp.bfloat16)

    lane_head = lax.broadcasted_iota(jnp.int32, (size, width), 1) // HD

    def one_brick(g, carry):
        brick = step * GROUP + g
        live = jnp.int32(0)
        for e in range(list_len):
            entry = entries[brick * list_len + e]

            @pl.when(entry >= 0)
            def _(entry=entry, live=live):
                tile = (entry // 2) * tile_dev + sends[entry]
                feat_s[pl.ds(pl.multiple_of(live * pixels, pixels), pixels), :] = cams[tile]

            live = live + (entry >= 0).astype(jnp.int32)
        here = pl.ds(pl.multiple_of(g * size, size), size)
        pair_count = (live + 1) // 2
        cap = jnp.where(live % 2 == 1, jnp.float32(-1e30), jnp.float32(3e38))
        for pairs in range(1, list_len // 2 + 1):

            @pl.when(pair_count == pairs)
            def _(pairs=pairs):
                n = pairs * 2 * pixels
                feats = feat_s[0:n, :]
                keys = dot(feats, w_key[...]).astype(jnp.bfloat16)
                values_t = dot(w_value_t[...], feats, NT).astype(jnp.bfloat16)
                query = query_s[here, :]
                outs = []
                for hp in range(width // HD // 2):
                    masked = [
                        jnp.where(lane_head == h, query, jnp.zeros_like(query))
                        for h in (2 * hp, 2 * hp + 1)
                    ]
                    scores = dot(keys, jnp.concatenate(masked, 0), NT)
                    scores = jnp.concatenate(
                        [scores[: n - pixels], jnp.minimum(scores[n - pixels :], cap)], 0
                    )
                    peak = jnp.max(scores, axis=0, keepdims=True)
                    raised = jnp.exp2((scores - peak) * log2_scale)
                    inverse = 1.0 / jnp.sum(raised, axis=0, keepdims=True)
                    weights = (raised * inverse).astype(jnp.bfloat16)
                    mixed = dot(values_t[2 * HD * hp : 2 * HD * (hp + 1), :], weights)
                    outs.append(mixed[:HD, :size])
                    outs.append(mixed[HD:, size:])
                att_s[here, :] = jnp.concatenate(outs, 0).T.astype(jnp.bfloat16)

        return carry

    lax.fori_loop(0, GROUP, one_brick, 0)

    residual = qin_s[...] + dot(att_s[...], w_attn_out[...])
    hidden = rms_norm(residual, gains[1:2, :]).astype(jnp.bfloat16)
    pre = dot(hidden, w_in[...])
    square = pre * pre
    root = 0.7978845608028654
    tanh = jnp.tanh(root * (pre + 0.044715 * (square * pre)))
    half = 0.5 * (1.0 + tanh)
    act = (pre * half).astype(jnp.bfloat16)
    new_state[...] = (
        (residual + dot(act, w_out[...])).astype(jnp.bfloat16).reshape(GROUP, size, width)
    )
    cotangent = cot[...].reshape(rows, width)
    d_act = dot(cotangent, w_out[...], NT)
    slope = half + (0.5 * root) * pre * (1.0 - tanh * tanh) * (1.0 + (3 * 0.044715) * square)
    d_pre = (d_act * slope).astype(jnp.bfloat16)
    grad_out[...] += dot(act, cotangent, TN)
    grad_in[...] += dot(hidden, d_pre, TN)


def local_step(
    sends, entries, shift, cams, behind, prev, vox, cot, gains, w_query, w_keyval, w_attn_out,
    w_in, w_out, interpret=False,
):
    bricks, size, width = prev.shape
    hidden = w_in.shape[1]
    rows = GROUP * size
    list_len = entries.shape[0] // bricks

    def whole(array):
        zeros = (0,) * array.ndim
        return pl.BlockSpec(array.shape, lambda i, *_: zeros, pipeline_mode=pl.Buffered(1))

    block = pl.BlockSpec((GROUP, size, width), lambda i, *_: (i, 0, 0))
    operands = (
        cams,
        behind,
        prev,
        vox,
        cot,
        gains,
        w_query,
        w_keyval[:, :width],
        w_keyval[:, width:].T,
        w_attn_out,
        w_in,
        w_out,
    )
    specs = [block if a is vox or a is cot else whole(a) for a in operands]
    return pl.pallas_call(
        step_kernel,
        out_shape=(
            jax.ShapeDtypeStruct((bricks, size, width), jnp.bfloat16),
            jax.ShapeDtypeStruct((width, hidden), jnp.float32),
            jax.ShapeDtypeStruct((hidden, width), jnp.float32),
        ),
        grid_spec=pltpu.PrefetchScalarGridSpec(
            num_scalar_prefetch=3,
            grid=(bricks // GROUP,),
            in_specs=specs,
            out_specs=(
                block,
                pl.BlockSpec((width, hidden), lambda i, *_: (0, 0)),
                pl.BlockSpec((hidden, width), lambda i, *_: (0, 0)),
            ),
            scratch_shapes=[
                pltpu.VMEM((rows, width), jnp.float32),
                pltpu.VMEM((rows, width), jnp.bfloat16),
                pltpu.VMEM((rows, width), jnp.bfloat16),
                pltpu.VMEM((list_len * cams.shape[1], width), jnp.bfloat16),
            ],
        ),
        compiler_params=pltpu.CompilerParams(vmem_limit_bytes=48 << 20),
        name="voxel_step",
        interpret=interpret,
    )(sends, entries, shift, *operands)


def on_device(
    cam_tiles,
    vox_embed,
    prev_state,
    tile_sends,
    brick_tiles,
    ego_shift,
    norm_gains,
    w_query,
    w_keyval,
    w_attn_out,
    w_in,
    w_out,
    grad_out,
):
    shards = lax.axis_size("brick")
    prev = prev_state[0]
    cams = lax.all_gather(cam_tiles[0, 0], "brick", axis=0, tiled=True)
    own_plan = lax.all_to_all(
        tile_sends[0, 0].reshape(shards, -1), "brick", 0, 0, tiled=True
    ).reshape(-1)
    behind = lax.ppermute(prev, "brick", [(i, i + 1) for i in range(shards - 1)])
    new_state, grad_w_in, grad_w_out = local_step(
        own_plan,
        brick_tiles[0, 0].reshape(-1),
        ego_shift[0],
        cams,
        behind,
        prev,
        vox_embed,
        grad_out[0],
        norm_gains,
        w_query,
        w_keyval,
        w_attn_out,
        w_in,
        w_out,
    )
    grad_w_in, grad_w_out = lax.psum((grad_w_in, grad_w_out), ("drive", "brick"))
    return (new_state[None], grad_w_in, grad_w_out)


def solution(mesh):
    return jax.shard_map(
        on_device,
        mesh=mesh,
        in_specs=(
            P("drive", None, "brick", None, None),
            P("brick", None, None),
            P("drive", "brick", None, None),
            P("drive", None, "brick", None),
            P("drive", None, "brick", None),
            P("drive", None),
            P(),
            P(),
            P(),
            P(),
            P(),
            P(),
            P("drive", "brick", None, None),
        ),
        out_specs=(P("drive", "brick", None, None), P(), P()),
        check_vma=False,
    )
```

```python
import functools

import jax
import jax.numpy as jnp
from jax import lax
from jax.experimental import pallas as pl
from jax.experimental.pallas import tpu as pltpu
from jax.sharding import PartitionSpec as P

HD = 32
GROUP = 4
NT = (((1,), (1,)), ((), ()))
TN = (((0,), (0,)), ((), ()))


def dot(a, b, dims=(((1,), (0,)), ((), ()))):
    return lax.dot_general(a, b, dims, preferred_element_type=jnp.float32)


def rms_norm(values, norm_gain):
    mean_sq = jnp.mean(values * values, axis=-1, keepdims=True)
    return values * lax.rsqrt(mean_sq + 1e-06) * norm_gain


def step_kernel(
    sends,
    entries,
    shift,
    cams,
    behind,
    prev,
    vox,
    cot,
    gains,
    w_query,
    w_key,
    w_value_t,
    w_attn_out,
    w_in,
    w_out,
    new_state,
    grads,
    qin_s,
    query_s,
    att_s,
    feat_s,
):
    step = pl.program_id(0)
    bricks = prev.shape[0]
    size = prev.shape[1]
    width = prev.shape[2]
    list_len = entries.shape[0] // bricks
    pixels = cams.shape[1]
    tile_dev = cams.shape[0] // (sends.shape[0] // 2)
    rows = GROUP * size
    log2_scale = 1.4426950408889634 / HD**0.5

    @pl.when(step == 0)
    def _():
        grads[...] = jnp.zeros_like(grads)
        feat_s[...] = jnp.zeros_like(feat_s)

    start = bricks - shift[0]
    for g in range(GROUP):
        at = start + step * GROUP + g
        from_behind = behind[jnp.minimum(at, bricks - 1)].astype(jnp.float32)
        from_own = prev[jnp.maximum(at - bricks, 0)].astype(jnp.float32)
        shifted = jnp.where(at < bricks, from_behind, from_own)
        q_in = vox[g].astype(jnp.float32) + shifted
        here = pl.ds(g * size, size)
        qin_s[here, :] = q_in
        normed = rms_norm(q_in, gains[0:1, :]).astype(jnp.bfloat16)
        query_s[here, :] = dot(normed, w_query[...]).astype(jnp.bfloat16)

    lane_head = lax.broadcasted_iota(jnp.int32, (size, width), 1) // HD

    def one_brick(g, carry):
        brick = step * GROUP + g
        live = jnp.int32(0)
        for e in range(list_len):
            entry = entries[brick * list_len + e]

            @pl.when(entry >= 0)
            def _(entry=entry, live=live):
                tile = (entry // 2) * tile_dev + sends[entry]
                feat_s[pl.ds(pl.multiple_of(live * pixels, pixels), pixels), :] = cams[tile]

            live = live + (entry >= 0).astype(jnp.int32)
        here = pl.ds(pl.multiple_of(g * size, size), size)
        pair_count = (live + 1) // 2
        cap = jnp.where(live % 2 == 1, jnp.float32(-1e30), jnp.float32(3e38))
        for pairs in range(1, list_len // 2 + 1):

            @pl.when(pair_count == pairs)
            def _(pairs=pairs):
                n = pairs * 2 * pixels
                feats = feat_s[0:n, :]
                keys = dot(feats, w_key[...]).astype(jnp.bfloat16)
                values_t = dot(w_value_t[...], feats, NT).astype(jnp.bfloat16)
                query = query_s[here, :]
                outs = []
                for hp in range(width // HD // 2):
                    masked = [
                        jnp.where(lane_head == h, query, jnp.zeros_like(query))
                        for h in (2 * hp, 2 * hp + 1)
                    ]
                    scores = dot(keys, jnp.concatenate(masked, 0), NT)
                    scores = jnp.concatenate(
                        [scores[: n - pixels], jnp.minimum(scores[n - pixels :], cap)], 0
                    )
                    peak = jnp.max(scores, axis=0, keepdims=True)
                    raised = jnp.exp2((scores - peak) * log2_scale)
                    inverse = 1.0 / jnp.sum(raised, axis=0, keepdims=True)
                    weights = (raised * inverse).astype(jnp.bfloat16)
                    mixed = dot(values_t[2 * HD * hp : 2 * HD * (hp + 1), :], weights)
                    outs.append(mixed[:HD, :size])
                    outs.append(mixed[HD:, size:])
                att_s[here, :] = jnp.concatenate(outs, 0).T.astype(jnp.bfloat16)

        return carry

    lax.fori_loop(0, GROUP, one_brick, 0)

    residual = qin_s[...] + dot(att_s[...], w_attn_out[...])
    hidden = rms_norm(residual, gains[1:2, :]).astype(jnp.bfloat16)
    pre = dot(hidden, w_in[...])
    square = pre * pre
    root = 0.7978845608028654
    tanh = jnp.tanh(root * (pre + 0.044715 * (square * pre)))
    half = 0.5 * (1.0 + tanh)
    act = (pre * half).astype(jnp.bfloat16)
    new_state[...] = (
        (residual + dot(act, w_out[...])).astype(jnp.bfloat16).reshape(GROUP, size, width)
    )
    cotangent = cot[...].reshape(rows, width)
    d_act = dot(cotangent, w_out[...], NT)
    slope = half + (0.5 * root) * pre * (1.0 - tanh * tanh) * (1.0 + (3 * 0.044715) * square)
    d_pre = (d_act * slope).astype(jnp.bfloat16)
    ff = act.shape[1]
    grads[:ff, :] += dot(act, cotangent, TN)
    grads[ff : ff + width, :] += dot(hidden, d_pre[:, :width], TN)
    grads[ff + width :, :] += dot(hidden, d_pre[:, width:], TN)


def local_step(
    sends, entries, shift, cams, behind, prev, vox, cot, gains, w_query, w_keyval, w_attn_out,
    w_in, w_out, interpret=False,
):
    bricks, size, width = prev.shape
    hidden = w_in.shape[1]
    rows = GROUP * size
    list_len = entries.shape[0] // bricks

    def whole(array):
        zeros = (0,) * array.ndim
        return pl.BlockSpec(array.shape, lambda i, *_: zeros, pipeline_mode=pl.Buffered(1))

    block = pl.BlockSpec((GROUP, size, width), lambda i, *_: (i, 0, 0))
    operands = (
        cams,
        behind,
        prev,
        vox,
        cot,
        gains,
        w_query,
        w_keyval[:, :width],
        w_keyval[:, width:].T,
        w_attn_out,
        w_in,
        w_out,
    )
    specs = [block if a is vox or a is cot else whole(a) for a in operands]
    return pl.pallas_call(
        step_kernel,
        out_shape=(
            jax.ShapeDtypeStruct((bricks, size, width), jnp.bfloat16),
            jax.ShapeDtypeStruct((2 * hidden, width), jnp.float32),
        ),
        grid_spec=pltpu.PrefetchScalarGridSpec(
            num_scalar_prefetch=3,
            grid=(bricks // GROUP,),
            in_specs=specs,
            out_specs=(
                block,
                pl.BlockSpec((2 * hidden, width), lambda i, *_: (0, 0)),
            ),
            scratch_shapes=[
                pltpu.VMEM((rows, width), jnp.float32),
                pltpu.VMEM((rows, width), jnp.bfloat16),
                pltpu.VMEM((rows, width), jnp.bfloat16),
                pltpu.VMEM((list_len * cams.shape[1], width), jnp.bfloat16),
            ],
        ),
        compiler_params=pltpu.CompilerParams(vmem_limit_bytes=48 << 20),
        name="voxel_step",
        interpret=interpret,
    )(sends, entries, shift, *operands)


SCATTER = ((1, 1), (16, 48), (48, 32), (2, 2), (4, 12))
WHOLE = (("brick", 12), ("drive", 1), ("drive", 3))


def swapped(value, axis, mask):
    pairs = [(i, i ^ mask) for i in range(lax.axis_size(axis))]
    return lax.ppermute(value, axis, pairs)


def parity(index, bits):
    return sum((index // (1 << k)) % 2 for k in range(6) if bits >> k & 1) % 2


def sum_over_devices(value):
    me = lax.axis_index("brick")
    for mask, bits in SCATTER:
        rows = value.shape[0] // 2
        side = parity(me, bits)
        kept = lax.dynamic_slice_in_dim(value, side * rows, rows, 0)
        sent = lax.dynamic_slice_in_dim(value, (1 - side) * rows, rows, 0)
        value = kept + swapped(sent, "brick", mask)
    for axis, mask in WHOLE:
        value = value + swapped(value, axis, mask)
    for mask, bits in reversed(SCATTER):
        other = swapped(value, "brick", mask)
        first = parity(me, bits) == 0
        value = jnp.where(
            first,
            jnp.concatenate([value, other], 0),
            jnp.concatenate([other, value], 0),
        )
    return value


def on_device(
    cam_tiles,
    vox_embed,
    prev_state,
    tile_sends,
    brick_tiles,
    ego_shift,
    norm_gains,
    w_query,
    w_keyval,
    w_attn_out,
    w_in,
    w_out,
    grad_out,
):
    shards = lax.axis_size("brick")
    prev = prev_state[0]
    cams = lax.all_gather(cam_tiles[0, 0], "brick", axis=0, tiled=True)
    own_plan = lax.all_to_all(
        tile_sends[0, 0].reshape(shards, -1), "brick", 0, 0, tiled=True
    ).reshape(-1)
    behind = lax.ppermute(prev, "brick", [(i, i + 1) for i in range(shards - 1)])
    new_state, grads = local_step(
        own_plan,
        brick_tiles[0, 0].reshape(-1),
        ego_shift[0],
        cams,
        behind,
        prev,
        vox_embed,
        grad_out[0],
        norm_gains,
        w_query,
        w_keyval,
        w_attn_out,
        w_in,
        w_out,
    )
    total = sum_over_devices(grads)
    width, hidden = w_in.shape
    grad_w_out = total[:hidden]
    grad_w_in = jnp.concatenate([total[hidden : hidden + width], total[hidden + width :]], 1)
    return (new_state[None], grad_w_in, grad_w_out)


def solution(mesh):
    return jax.shard_map(
        on_device,
        mesh=mesh,
        in_specs=(
            P("drive", None, "brick", None, None),
            P("brick", None, None),
            P("drive", "brick", None, None),
            P("drive", None, "brick", None),
            P("drive", None, "brick", None),
            P("drive", None),
            P(),
            P(),
            P(),
            P(),
            P(),
            P(),
            P("drive", "brick", None, None),
        ),
        out_specs=(P("drive", "brick", None, None), P(), P()),
        check_vma=False,
    )
```

```python
import functools

import jax
import jax.numpy as jnp
from jax import lax
from jax.experimental import pallas as pl
from jax.experimental.pallas import tpu as pltpu
from jax.sharding import PartitionSpec as P

HD = 32
GROUP = 4
NT = (((1,), (1,)), ((), ()))
TN = (((0,), (0,)), ((), ()))


def dot(a, b, dims=(((1,), (0,)), ((), ()))):
    return lax.dot_general(a, b, dims, preferred_element_type=jnp.float32)


def rms_norm(values, norm_gain):
    mean_sq = jnp.mean(values * values, axis=-1, keepdims=True)
    return values * lax.rsqrt(mean_sq + 1e-06) * norm_gain


def step_kernel(sources, me, entries, shift, *refs):
    brick_kernel(sources, me, entries, shift, refs[: len(sources)], *refs[len(sources) :])


def shard_of(me, source):
    x, z, core = me // 16, me // 2 % 8, me % 2
    mask_x, mask_z, step_z, swap = source
    return (x ^ mask_x) * 16 + (((z ^ mask_z) + step_z) % 8) * 2 + (core ^ swap)


def brick_kernel(
    sources,
    me,
    entries,
    shift,
    pieces,
    behind,
    prev,
    vox,
    cot,
    gains,
    w_query,
    w_key,
    w_value_t,
    w_attn_out,
    w_in,
    w_out,
    new_state,
    grads,
    qin_s,
    query_s,
    att_s,
    feat_s,
    cams,
    plan_v,
    plan,
    sem,
):
    step = pl.program_id(0)
    bricks = prev.shape[0]
    size = prev.shape[1]
    width = prev.shape[2]
    list_len = entries.shape[0] // bricks
    pixels = feat_s.shape[0] // list_len
    own = me[0]
    rows = GROUP * size
    log2_scale = 1.4426950408889634 / HD**0.5

    @pl.when(step == 0)
    def _():
        for piece, (first_row, blocks) in zip(pieces, sources):
            for at, source in enumerate(blocks):
                pltpu.make_async_copy(
                    piece.at[at],
                    cams.at[shard_of(own, source), pl.ds(first_row, piece.shape[1]), :],
                    sem,
                ).start()
        grads[...] = jnp.zeros_like(grads)
        feat_s[...] = jnp.zeros_like(feat_s)

    start = bricks - shift[0]
    for g in range(GROUP):
        at = start + step * GROUP + g
        from_behind = behind[jnp.minimum(at, bricks - 1)].astype(jnp.float32)
        from_own = prev[jnp.maximum(at - bricks, 0)].astype(jnp.float32)
        shifted = jnp.where(at < bricks, from_behind, from_own)
        q_in = vox[g].astype(jnp.float32) + shifted
        here = pl.ds(g * size, size)
        qin_s[here, :] = q_in
        normed = rms_norm(q_in, gains[0:1, :]).astype(jnp.bfloat16)
        query_s[here, :] = dot(normed, w_query[...]).astype(jnp.bfloat16)

    @pl.when(step == 0)
    def _():
        pltpu.make_async_copy(cams, cams, sem).wait()
        table = cams[:, pl.ds(FIRST * pixels, 16), pl.ds(0, 128)].astype(jnp.float32)
        plan_v[...] = jnp.sum(table, axis=1).astype(jnp.int32)
        pltpu.sync_copy(plan_v, plan)

    lane_head = lax.broadcasted_iota(jnp.int32, (size, width), 1) // HD

    def one_brick(g, carry):
        brick = step * GROUP + g
        live = jnp.int32(0)
        for e in range(list_len):
            entry = entries[brick * list_len + e]

            @pl.when(entry >= 0)
            def _(entry=entry, live=live):
                local = plan[entry // 2, own * 2 + entry % 2]
                row = local * pixels + jnp.where(local >= FIRST, 16, 0)
                feat_s[pl.ds(pl.multiple_of(live * pixels, pixels), pixels), :] = cams[
                    entry // 2, pl.ds(pl.multiple_of(row, 16), pixels), :
                ]

            live = live + (entry >= 0).astype(jnp.int32)
        here = pl.ds(pl.multiple_of(g * size, size), size)
        pair_count = (live + 1) // 2
        cap = jnp.where(live % 2 == 1, jnp.float32(-1e30), jnp.float32(3e38))
        for pairs in range(1, list_len // 2 + 1):

            @pl.when(pair_count == pairs)
            def _(pairs=pairs):
                n = pairs * 2 * pixels
                feats = feat_s[0:n, :]
                keys = dot(feats, w_key[...]).astype(jnp.bfloat16)
                values_t = dot(w_value_t[...], feats, NT).astype(jnp.bfloat16)
                query = query_s[here, :]
                outs = []
                for hp in range(width // HD // 2):
                    masked = [
                        jnp.where(lane_head == h, query, jnp.zeros_like(query))
                        for h in (2 * hp, 2 * hp + 1)
                    ]
                    scores = dot(keys, jnp.concatenate(masked, 0), NT)
                    scores = jnp.concatenate(
                        [scores[: n - pixels], jnp.minimum(scores[n - pixels :], cap)], 0
                    )
                    peak = jnp.max(scores, axis=0, keepdims=True)
                    raised = jnp.exp2((scores - peak) * log2_scale)
                    inverse = 1.0 / jnp.sum(raised, axis=0, keepdims=True)
                    weights = (raised * inverse).astype(jnp.bfloat16)
                    mixed = dot(values_t[2 * HD * hp : 2 * HD * (hp + 1), :], weights)
                    outs.append(mixed[:HD, :size])
                    outs.append(mixed[HD:, size:])
                att_s[here, :] = jnp.concatenate(outs, 0).T.astype(jnp.bfloat16)

        return carry

    lax.fori_loop(0, GROUP, one_brick, 0)

    residual = qin_s[...] + dot(att_s[...], w_attn_out[...])
    hidden = rms_norm(residual, gains[1:2, :]).astype(jnp.bfloat16)
    pre = dot(hidden, w_in[...])
    square = pre * pre
    root = 0.7978845608028654
    tanh = jnp.tanh(root * (pre + 0.044715 * (square * pre)))
    half = 0.5 * (1.0 + tanh)
    act = (pre * half).astype(jnp.bfloat16)
    new_state[...] = (
        (residual + dot(act, w_out[...])).astype(jnp.bfloat16).reshape(GROUP, size, width)
    )
    cotangent = cot[...].reshape(rows, width)
    d_act = dot(cotangent, w_out[...], NT)
    slope = half + (0.5 * root) * pre * (1.0 - tanh * tanh) * (1.0 + (3 * 0.044715) * square)
    d_pre = (d_act * slope).astype(jnp.bfloat16)
    ff = act.shape[1]
    grads[:ff, :] += dot(act, cotangent, TN)
    grads[ff : ff + width, :] += dot(hidden, d_pre[:, :width], TN)
    grads[ff + width :, :] += dot(hidden, d_pre[:, width:], TN)


def local_step(
    me, entries, shift, pieces, sources, pixels, behind, prev, vox, cot, gains, w_query, w_keyval, w_attn_out,
    w_in, w_out, interpret=False,
):
    bricks, size, width = prev.shape
    hidden = w_in.shape[1]
    rows = GROUP * size
    list_len = entries.shape[0] // bricks

    def whole(array):
        zeros = (0,) * array.ndim
        return pl.BlockSpec(array.shape, lambda i, *_: zeros, pipeline_mode=pl.Buffered(1))

    block = pl.BlockSpec((GROUP, size, width), lambda i, *_: (i, 0, 0))
    operands = (
        behind,
        prev,
        vox,
        cot,
        gains,
        w_query,
        w_keyval[:, :width],
        w_keyval[:, width:].T,
        w_attn_out,
        w_in,
        w_out,
    )
    specs = [pl.BlockSpec(memory_space=pltpu.HBM)] * len(pieces)
    specs += [block if a is vox or a is cot else whole(a) for a in operands]
    shards = sum(len(blocks) for first_row, blocks in sources if first_row == 0)
    per_shard = sum({f: p.shape[1] for p, (f, _) in zip(pieces, sources)}.values())
    return pl.pallas_call(
        functools.partial(step_kernel, sources),
        out_shape=(
            jax.ShapeDtypeStruct((bricks, size, width), jnp.bfloat16),
            jax.ShapeDtypeStruct((2 * hidden, width), jnp.float32),
        ),
        grid_spec=pltpu.PrefetchScalarGridSpec(
            num_scalar_prefetch=3,
            grid=(bricks // GROUP,),
            in_specs=specs,
            out_specs=(
                block,
                pl.BlockSpec((2 * hidden, width), lambda i, *_: (0, 0)),
            ),
            scratch_shapes=[
                pltpu.VMEM((rows, width), jnp.float32),
                pltpu.VMEM((rows, width), jnp.bfloat16),
                pltpu.VMEM((rows, width), jnp.bfloat16),
                pltpu.VMEM((list_len * pixels, width), jnp.bfloat16),
                pltpu.VMEM((shards, per_shard, width), jnp.bfloat16),
                pltpu.VMEM((shards, 128), jnp.int32),
                pltpu.SMEM((shards, 128), jnp.int32),
                pltpu.SemaphoreType.DMA,
            ],
        ),
        compiler_params=pltpu.CompilerParams(vmem_limit_bytes=60 * 1024 * 1024),
        name="voxel_step",
        interpret=interpret,
    )(me, entries, shift, *pieces, *operands)


SCATTER = ((1, 1), (16, 48), (48, 32), (2, 2), (4, 12))
WHOLE = (("brick", 12), ("drive", 1), ("drive", 3))


def swapped(value, axis, mask):
    pairs = [(i, i ^ mask) for i in range(lax.axis_size(axis))]
    return lax.ppermute(value, axis, pairs)


def parity(index, bits):
    return sum((index // (1 << k)) % 2 for k in range(6) if bits >> k & 1) % 2


def sum_over_devices(value):
    me = lax.axis_index("brick")
    for mask, bits in SCATTER:
        rows = value.shape[0] // 2
        side = parity(me, bits)
        kept = lax.dynamic_slice_in_dim(value, side * rows, rows, 0)
        sent = lax.dynamic_slice_in_dim(value, (1 - side) * rows, rows, 0)
        value = kept + swapped(sent, "brick", mask)
    for axis, mask in WHOLE:
        value = value + swapped(value, axis, mask)
    for mask, bits in reversed(SCATTER):
        other = swapped(value, "brick", mask)
        first = parity(me, bits) == 0
        value = jnp.where(
            first,
            jnp.concatenate([value, other], 0),
            jnp.concatenate([other, value], 0),
        )
    return value


FIRST = 4


def along_z(value, step):
    def target(i):
        return i // 16 * 16 + (i // 2 + step) % 8 * 2 + i % 2

    return lax.ppermute(value, "brick", [(i, target(i)) for i in range(64)])


def gathered(tiles, sends):
    width = tiles.shape[-1]
    table = jnp.pad(sends.astype(tiles.dtype), ((0, 15), (0, width - sends.shape[1])))
    first = jnp.concatenate([tiles[:FIRST].reshape(-1, width), table], 0)[None]
    found = []

    first = jnp.concatenate([first, swapped(first, "brick", 16)], 0)
    first = jnp.concatenate([first, swapped(first, "brick", 48)], 0)
    xs = (0, 1, 3, 2)
    found.append((first, 0, [(m, 0, 0, 0) for m in xs]))
    for way, count in ((1, 3), (-1, 4)):
        block = first
        for k in range(1, count + 1):
            block = along_z(block, way)
            found.append((block, 0, [(m, 0, -way * k, 0) for m in xs]))

    if FIRST < tiles.shape[0]:
        row = first.shape[1]
        second = tiles[FIRST:].reshape(1, -1, width)
        for mask in (2, 4, 12):
            second = jnp.concatenate([second, swapped(second, "brick", mask)], 0)
        zs = (0, 1, 2, 3, 6, 7, 4, 5)
        third = swapped(second, "brick", 16)
        for block, m in (
            (second, 0),
            (third, 1),
            (swapped(second, "brick", 48), 3),
            (swapped(third, "brick", 48), 2),
        ):
            found.append((block, row, [(m, n, 0, 0) for n in zs]))

    found += [
        (swapped(block, "brick", 1), row, [(a, b, c, 1) for a, b, c, _ in blocks])
        for block, row, blocks in found
    ]
    return [f[0] for f in found], [f[1:] for f in found]


def on_device(
    cam_tiles,
    vox_embed,
    prev_state,
    tile_sends,
    brick_tiles,
    ego_shift,
    norm_gains,
    w_query,
    w_keyval,
    w_attn_out,
    w_in,
    w_out,
    grad_out,
):
    shards = lax.axis_size("brick")
    prev = prev_state[0]
    behind = lax.ppermute(prev, "brick", [(i, i + 1) for i in range(shards - 1)])
    pixels = cam_tiles.shape[3]
    pieces, sources = gathered(cam_tiles[0, 0], tile_sends[0, 0])
    new_state, grads = local_step(
        lax.axis_index("brick").reshape(1),
        brick_tiles[0, 0].reshape(-1),
        ego_shift[0],
        pieces,
        sources,
        pixels,
        behind,
        prev,
        vox_embed,
        grad_out[0],
        norm_gains,
        w_query,
        w_keyval,
        w_attn_out,
        w_in,
        w_out,
    )
    total = sum_over_devices(grads)
    width, hidden = w_in.shape
    grad_w_out = total[:hidden]
    grad_w_in = jnp.concatenate([total[hidden : hidden + width], total[hidden + width :]], 1)
    return (new_state[None], grad_w_in, grad_w_out)


def solution(mesh):
    return jax.shard_map(
        on_device,
        mesh=mesh,
        in_specs=(
            P("drive", None, "brick", None, None),
            P("brick", None, None),
            P("drive", "brick", None, None),
            P("drive", None, "brick", None),
            P("drive", None, "brick", None),
            P("drive", None),
            P(),
            P(),
            P(),
            P(),
            P(),
            P(),
            P("drive", "brick", None, None),
        ),
        out_specs=(P("drive", "brick", None, None), P(), P()),
        check_vma=False,
    )
```
